32 devices in a mesh: dp: 16 (over z, y, x), section: 2 (over core).
Axes of the slice: x: 2, y: 2, z: 4, core: 2. Of those that a mesh axis runs over, the one named last changes fastest.
Arguments:
- section_inputs: bfloat16 [2, 2, 2048, 2048], P('section', None, 'dp'), may hold values from -6 to 6
- mix_weight: bfloat16 [2, 2048, 2048], P('section'), may hold values from -0.0625 to 0.0625
- norm_gain: float32 [2, 2048], P('section'), may hold values from 0.5 to 1.5
- out_cotangent: bfloat16 [2, 2048, 2048], P(None, 'dp'), may hold values from -6 to 6
- positions: int32 [2, 2048], P(None, 'dp'), may hold values from 0 to 1023
Outputs:
- grad_inputs: bfloat16 [2, 2, 2048, 2048], P('section', None, 'dp')
- grad_weight: float32 [2, 2048, 2048], P('section', 'dp')
- grad_gain: float32 [2, 2048], P('section', 'dp')
The draws below stay inside these ranges and needn't reach their ends.
Inputs may be any that keep to these rules, and one draw needn't show every extreme that they name: `positions`: depth index of a token within its tile.
All inputs are finite; a program needn't handle non-finite values.
Results may differ from the reference program's by a relative error of at most 0.017.
Values may be sent and summed in bfloat16 or wider, within the bound.
A program may use at most 128 MiB of HBM per device.

```python
import math
import jax
import jax.numpy as jnp
from jax import lax

CHANNELS = 2048
MICROBATCH = 2
TOKENS_MB = 128
DEPTH = 1024
SECTIONS = 2
TOKENS = 2048
N_DP = 16


def place_ends(drawn, rng, low, high):
    longest = drawn.shape.index(max(drawn.shape))
    spots = []
    for shift in (0, 1):
        where = [jax.random.randint(jax.random.fold_in(rng, axis), (), 0, length) for axis, length in enumerate(drawn.shape)]
        where[longest] = (where[longest] + shift) % drawn.shape[longest]
        spots.append(tuple(where))
    return drawn.at[spots[0]].set(low).at[spots[1]].set(high)


def spiked(values, own_key, source, target, shards_of, factor):
    def block_of(axis_at):
        return (jnp.arange(values.shape[axis_at]) // (values.shape[axis_at] // shards_of)).reshape((-1,) + (1,) * (values.ndim - 1 - axis_at))

    near = jax.random.permutation(own_key, shards_of)[block_of(target)]
    far = (block_of(target) + shards_of // 2) % shards_of
    return jnp.where((block_of(source) == near) | (block_of(source) == far), factor * values, values)


def block_scale(own_key, extent, split, low, largest):
    level, own = 1.0, jax.random.fold_in(own_key, 6)
    for axis_at, shards_of in split:
        draws = jnp.exp(jax.random.uniform(jax.random.fold_in(own, axis_at), (shards_of,), jnp.float32, low / len(split), largest / len(split)))
        level = level * jnp.repeat(draws, extent[axis_at] // shards_of).reshape([-1 if axis == axis_at else 1 for axis in range(len(extent))])
    return level


def centred(rng, shape, spread, limit, shards=(), dtype=jnp.bfloat16):
    array = spread * jax.random.normal(rng, shape, jnp.float32)
    if shards:
        array = array * block_scale(rng, shape, shards, -0.22, 0.18)
    return jnp.clip(array, -limit, limit).astype(dtype)


def heavy_noise(stream_key, dims, deviation, bound, pieces, heavy, dtype=jnp.bfloat16):
    entries = deviation * jax.random.normal(stream_key, dims, jnp.float32)
    if pieces:
        entries = entries * block_scale(stream_key, dims, pieces, -0.22, 0.18)
    return jnp.clip(spiked(entries, jax.random.fold_in(stream_key, 3), *heavy), -bound, bound).astype(dtype)


def setup_inputs(seed: int = 0) -> dict:
    streams_of = jax.random.split(jax.random.key(seed), 6)
    section_inputs = heavy_noise(streams_of[0], (SECTIONS, MICROBATCH, TOKENS, CHANNELS), 1.0, 6.0, ((0, 2), (2, 16)), (2, 3, 16, 2.0))
    mix_weight = centred(streams_of[1], (SECTIONS, CHANNELS, CHANNELS), (4 * CHANNELS) ** -0.5, 0.0625, ((0, 2),))
    norm_gain = jnp.clip(1.0 + 0.1 * jax.random.normal(streams_of[2], (SECTIONS, CHANNELS), jnp.float32), 0.5, 1.5)
    out_cotangent = centred(streams_of[3], (MICROBATCH, TOKENS, CHANNELS), 1.0, 6.0, ((1, 16),))
    positions = place_ends(jax.random.randint(streams_of[4], (MICROBATCH, TOKENS), 0, DEPTH), jax.random.fold_in(streams_of[4], 1), 0, DEPTH - 1).astype(jnp.int32)
    return dict(section_inputs=section_inputs, mix_weight=mix_weight, norm_gain=norm_gain, out_cotangent=out_cotangent, positions=positions)


def section_back(inputs, grad_out, factor, gain_vec, weight_mat):
    inputs_f = inputs.astype(jnp.float32)
    inv_rms = lax.rsqrt(lax.optimization_barrier(jnp.mean(inputs_f * inputs_f, axis=-1, keepdims=True)) + 1e-06)
    normed = inputs_f * inv_rms * gain_vec
    activation, gelu_back = jax.vjp(jax.nn.gelu, normed)
    upstream = (factor[:, None] * grad_out.astype(jnp.float32)).astype(jnp.bfloat16)
    back = lax.dot_general(upstream, weight_mat, (((1,), (1,)), ((), ())), preferred_element_type=jnp.float32)
    grad_norm = gelu_back(back)[0]
    scaled = grad_norm * gain_vec
    projected = lax.optimization_barrier(jnp.mean(scaled * inputs_f, axis=-1, keepdims=True))
    delta = inv_rms * scaled - inputs_f * (inv_rms * inv_rms * inv_rms) * projected
    grad_in = (grad_out.astype(jnp.float32) + delta).astype(jnp.bfloat16)
    gain_term = lax.optimization_barrier(jnp.sum(grad_norm * inputs_f * inv_rms, axis=0))
    return (grad_in, upstream, activation.astype(jnp.bfloat16), gain_term)

def weight_sum(activation, upstream):
    act_blocks = activation.reshape(MICROBATCH * N_DP, TOKENS_MB, CHANNELS)
    up_blocks = upstream.reshape(MICROBATCH * N_DP, TOKENS_MB, CHANNELS)

    def add_block(carry, pair):
        term = lax.dot_general(pair[0], pair[1], (((0,), (0,)), ((), ())), preferred_element_type=jnp.float32)
        rounded = lax.optimization_barrier(term.astype(jnp.bfloat16))
        return (carry + rounded.astype(jnp.float32), None)
    total, _ = lax.scan(add_block, jnp.zeros((CHANNELS, CHANNELS), jnp.float32), (act_blocks, up_blocks))
    return total

def reference(section_inputs, mix_weight, norm_gain, out_cotangent, positions):
    total = MICROBATCH * TOKENS
    depth_gain = 1.0 + 0.5 * jnp.sin(2.0 * math.pi * positions.reshape(total).astype(jnp.float32) / DEPTH)
    grad_out = out_cotangent.reshape(total, CHANNELS)
    grads = []
    weights = []
    gains = []
    for section_idx in range(SECTIONS - 1, -1, -1):
        inputs = section_inputs[section_idx].reshape(total, CHANNELS)
        grad_in, upstream, activation, gain_term = section_back(inputs, grad_out, depth_gain, norm_gain[section_idx], mix_weight[section_idx])
        weights.append(weight_sum(activation, upstream))
        gains.append(gain_term)
        grads.append(grad_in.reshape(MICROBATCH, TOKENS, CHANNELS))
        grad_out = grad_in
    grads = grads[::-1]
    weights = weights[::-1]
    gains = gains[::-1]
    return (jnp.stack(grads), jnp.stack(weights), jnp.stack(gains))
```

```python
import functools
import math

import jax
import jax.numpy as jnp
from jax import lax
from jax.experimental import pallas as pl
from jax.experimental.pallas import tpu as pltpu
from jax.sharding import PartitionSpec as P

DEPTH = 1024
MESH = pl.DeviceIdType.MESH
F32 = jnp.float32
BF16 = jnp.bfloat16
ROOT = math.sqrt(2.0 / math.pi)
CUBE = 0.044715
CHUNKS = 4


def contract(a, b, dims):
    return lax.dot_general(a, b, (dims, ((), ())), preferred_element_type=F32)


def block_order(planes, chunks):
    pairs = planes // 2
    first = [(i, k) for i in range(pairs) for k in range(2)]
    return first + [(i, k) for k in range(2, chunks) for i in range(pairs)]


def back_kernel(
    planes, sections, x_hbm, w_hbm, cot_hbm, gain_hbm, pos_hbm, out_ref, gain_out, grads_ref,
    x_ref, w_ref, g_ref, gain_ref, pos_ref, slope, tmp, eye_ref, act_ref, up_ref, q_ref, m_ref,
    proj, gath_a, gath_u, part, from_left, from_right, to_right, to_left, swap_out, swap_in,
    gain_own, gain_in, gain_mid, gain_sum, gain_z,
    in_sem, sec_send, sec_recv, u_send, u_recv, a_send, a_recv, s_send, s_recv,
    r_send, r_recv, l_send, l_recv, g_send, g_recv,
):
    me = lax.axis_index("dp")
    sec = lax.axis_index("section")
    last = sections - 1
    total = planes * 4
    x = lax.rem(me, 2)
    y = lax.rem(me // 2, 2)
    z = me // 4
    xn = me + 1 - 2 * x
    yn = me + 2 - 4 * y
    tokens, channels = x_ref.shape
    half = channels // 2
    rows = half // planes
    share = rows // 2
    micro, tok_mb = pos_ref.shape
    step_rows = 16
    width = min(256, channels)
    part_cols = half // CHUNKS
    pairs = planes // 2

    load_x = pltpu.make_async_copy(x_hbm, x_ref, in_sem.at[0])
    load_w = pltpu.make_async_copy(w_hbm, w_ref, in_sem.at[1])
    load_g = pltpu.make_async_copy(cot_hbm, g_ref, in_sem.at[2])
    load_gain = pltpu.make_async_copy(gain_hbm, gain_ref, in_sem.at[3])
    load_pos = pltpu.make_async_copy(pos_hbm, pos_ref, in_sem.at[4])
    load_pos.start()

    @pl.when(sec == last)
    def _():
        load_g.start()

    load_x.start()
    load_gain.start()
    load_w.start()

    def copy(src, dst, send, recv, to):
        return pltpu.make_async_remote_copy(
            src_ref=src, dst_ref=dst, send_sem=send, recv_sem=recv,
            device_id={"dp": to}, device_id_type=MESH,
        )

    barrier = pltpu.get_barrier_semaphore()
    z_peers = [lax.rem(me + 4 * step, total) for step in range(1, planes)]
    for peer in [xn, yn] + z_peers:
        pl.semaphore_signal(barrier, inc=1, device_id={"dp": peer}, device_id_type=MESH)

    @pl.when(sec > 0)
    def _():
        pl.semaphore_signal(barrier, inc=1, device_id={"section": sec - 1}, device_id_type=MESH)

    @pl.when(sec < last)
    def _():
        pl.semaphore_signal(barrier, inc=1, device_id={"section": sec + 1}, device_id_type=MESH)

    proj[...] = jnp.zeros_like(proj)
    at_row = lax.broadcasted_iota(jnp.int32, (rows, rows), 0)
    at_col = lax.broadcasted_iota(jnp.int32, (rows, rows), 1)
    eye_ref[...] = jnp.where(at_row == at_col, 1.0, 0.0).astype(BF16)
    with jax.named_scope("w_pos"):
        load_pos.wait()
    factor = 1.0 + 0.5 * jnp.sin(2.0 * math.pi * pos_ref[...].astype(F32) / DEPTH)
    for mb in range(micro):
        m_ref[mb * tok_mb:(mb + 1) * tok_mb, :] = jnp.transpose(
            jnp.broadcast_to(factor[mb:mb + 1, :], (128, tok_mb))
        )

    ux = [
        copy(up_ref.at[(1 - x) * CHUNKS + k], gath_u.at[k], u_send.at[k], u_recv.at[k], xn)
        for k in range(CHUNKS)
    ]
    uy = [
        copy(
            up_ref.at[x * CHUNKS + k], gath_u.at[CHUNKS + k],
            u_send.at[CHUNKS + k], u_recv.at[CHUNKS + k], yn,
        )
        for k in range(CHUNKS)
    ]
    ud = [
        copy(
            gath_u.at[k], gath_u.at[2 * CHUNKS + k],
            u_send.at[2 * CHUNKS + k], u_recv.at[2 * CHUNKS + k], yn,
        )
        for k in range(CHUNKS)
    ]
    spans = [pl.ds(b * rows, rows) for b in range(planes)]
    ax = [
        copy(act_ref.at[y, spans[b]], gath_a.at[0, spans[b]], a_send.at[b], a_recv.at[b], xn)
        for b in range(planes)
    ]
    ay = [
        copy(
            act_ref.at[1 - y, spans[b]], gath_a.at[1, spans[b]],
            a_send.at[planes + b], a_recv.at[planes + b], yn,
        )
        for b in range(planes)
    ]
    ad = [
        copy(
            gath_a.at[1, spans[b]], gath_a.at[2, spans[b]],
            a_send.at[2 * planes + b], a_recv.at[2 * planes + b], xn,
        )
        for b in range(planes)
    ]
    gain_x = copy(gain_own, gain_in.at[0], g_send.at[0], g_recv.at[0], xn)
    gain_y = copy(gain_mid, gain_in.at[1], g_send.at[1], g_recv.at[1], yn)

    def relay(mb):
        span = pl.ds(mb * tok_mb, tok_mb)
        return pltpu.make_async_remote_copy(
            src_ref=grads_ref.at[span, :], dst_ref=g_ref.at[span, :],
            send_sem=sec_send.at[mb], recv_sem=sec_recv.at[mb],
            device_id={"section": jnp.maximum(sec - 1, 0)}, device_id_type=MESH,
        )

    arrived = set()

    def arrive(name, sent):
        if name not in arrived:
            arrived.add(name)
            with jax.named_scope("w_" + name):
                sent.wait_recv()

    def forward_u(k):
        arrive("ux%d" % k, ux[k])
        ud[k].start()

    def forward_a(b):
        arrive("ay%d" % b, ay[b])
        ad[b].start()

    def upstream(mb):
        @pl.loop(mb * (tok_mb // step_rows), (mb + 1) * (tok_mb // step_rows))
        def _(i):
            r = pl.ds(pl.multiple_of(i * step_rows, step_rows), step_rows)
            m = m_ref[r, :]
            for c in range(channels // 128):
                at = c * 128
                g = g_ref[r, at:at + 128].astype(F32)
                low = at % part_cols
                up_ref[at // part_cols, r, low:low + 128] = (m * g).astype(BF16)

    @pl.when(sec == last)
    def _():
        with jax.named_scope("w_g"):
            load_g.wait()
        for mb in range(micro):
            upstream(mb)

    beside = jnp.minimum(sec, 1) + jnp.minimum(last - sec, 1)
    with jax.named_scope("barrier"):
        pl.semaphore_wait(barrier, 1 + planes + beside)

    @pl.when(sec == last)
    def _():
        ux[0].start()
        uy[0].start()

    with jax.named_scope("w_x"):
        load_x.wait()
        load_gain.wait()

    @pl.loop(0, tokens // step_rows)
    def _(i):
        r = pl.ds(pl.multiple_of(i * step_rows, step_rows), step_rows)
        square = jnp.zeros((step_rows, rows), F32)
        for c in range(channels // rows):
            xc = x_ref[r, c * rows:(c + 1) * rows].astype(F32)
            square = square + xc * xc
        q = lax.rsqrt(jnp.sum(square, axis=-1, keepdims=True) / channels + 1e-06)
        q_ref[r, :] = jnp.broadcast_to(q, (step_rows, 128))

    tall = 32

    def activate(b):
        @pl.loop(0, tokens // tall)
        def _(i):
            r = pl.ds(pl.multiple_of(i * tall, tall), tall)
            q = q_ref[r, :]
            for c in range(2 * rows // 128):
                at = 2 * b * rows + c * 128
                cols = slice(at, at + 128)
                low = c * 128 % rows
                n = x_ref[r, cols].astype(F32) * q * gain_ref[:, cols]
                n2 = n * n
                th = jnp.tanh(ROOT * (n + CUBE * (n2 * n)))
                cdf = 0.5 * (1.0 + th)
                tmp[c * 128 // rows, r, low:low + 128] = (n * cdf).astype(BF16)
                slope[r, cols] = cdf + (0.5 * ROOT) * n * (1.0 - th * th) * (1.0 + (3.0 * CUBE) * n2)

        for side in range(2):
            act_ref[side, spans[b], :] = contract(eye_ref[...], tmp[side], ((1,), (1,))).astype(BF16)

    order = []
    for i in range(pairs):
        order += [i, planes - 1 - i]
    for n, b in enumerate(order):
        activate(b)
        if n < 2:
            @pl.when(sec == last)
            def _():
                ay[b].start()
                ax[b].start()

    @pl.when(sec < last)
    def _():
        for mb in range(micro):
            with jax.named_scope("w_relay%d" % mb):
                relay(mb).wait_recv()
            upstream(mb)
        ux[0].start()
        uy[0].start()
        for b in order[:2]:
            ay[b].start()
            ax[b].start()

    forward_u(0)
    with jax.named_scope("w_w"):
        load_w.wait()

    def back_columns(start, stop):
        @pl.loop(start, stop)
        def _(c):
            cols = pl.ds(pl.multiple_of(c * width, width), width)
            back = jnp.zeros((tokens, width), F32)
            for h in range(2 * CHUNKS):
                back = back + contract(
                    up_ref[h], w_ref[cols, h * part_cols:(h + 1) * part_cols], ((1,), (1,))
                )
            lanes = proj[...]
            q = q_ref[...]
            for k in range(width // 128):
                piece = pl.ds(pl.multiple_of(c * width + k * 128, 128), 128)
                grad_norm = back[:, k * 128:(k + 1) * 128] * slope[:, piece]
                xc = x_ref[:, piece].astype(F32)
                scaled = grad_norm * gain_ref[:, piece]
                slope[:, piece] = scaled
                lanes = lanes + scaled * xc
                gain_own[:, piece] = jnp.sum(grad_norm * xc * q, axis=0, keepdims=True)
            proj[...] = lanes

    steps = channels // width
    back_columns(0, steps // 4)
    forward_a(order[0])
    back_columns(steps // 4, steps // 2)
    forward_a(order[1])
    ux[1].start()
    for b in order[2:]:
        ay[b].start()
        ax[b].start()
    uy[1].start()
    back_columns(steps // 2, steps)
    gain_x.start()

    for mb in range(micro):
        @pl.loop(mb * (tok_mb // step_rows), (mb + 1) * (tok_mb // step_rows))
        def _(i):
            r = pl.ds(pl.multiple_of(i * step_rows, step_rows), step_rows)
            q = q_ref[r, :]
            along = jnp.sum(proj[r, :], axis=-1, keepdims=True) / channels
            pull = (q * q * q) * jnp.broadcast_to(along, (step_rows, 128))
            for c in range(channels // 128):
                cols = slice(c * 128, (c + 1) * 128)
                delta = q * slope[r, cols] - x_ref[r, cols].astype(F32) * pull
                grads_ref[r, cols] = (g_ref[r, cols].astype(F32) + delta).astype(BF16)

        @pl.when(sec > 0)
        def _():
            relay(mb).start()

    z_next = lax.rem(me + 4, total)
    z_prev = lax.rem(me + total - 4, total)

    def right(at):
        return copy(to_right.at[at], from_left.at[at], r_send.at[at], r_recv.at[at], z_next)

    def left(at):
        return copy(to_left.at[at], from_right.at[at], l_send.at[at], l_recv.at[at], z_prev)

    def products(i, k):
        for b in (i, planes - 1 - i):
            arrive("ax%d" % b, ax[b])
            arrive("ad%d" % b, ad[b])
        arrive("uy%d" % k, uy[k])
        arrive("ud%d" % k, ud[k])

        @pl.loop(0, 2)
        def _(n):
            b = i + n * (planes - 1 - 2 * i)
            span = pl.ds(pl.multiple_of(b * rows, rows), rows)
            inner = ((1,), (0,))
            term = contract(act_ref[y, span, :], up_ref[x * CHUNKS + k], inner)
            for slot in range(3):
                term = term + contract(
                    gath_a[slot, span, :], gath_u[slot * CHUNKS + k], inner
                )
            part[k * planes + b] = term

    def stage(h, i, k):
        near = planes - 1 - h

        @pl.when(z == h)
        def _():
            for d in (planes - 1 - i, i):
                if d > h:
                    at = k * planes + d
                    if h > 0:
                        with jax.named_scope("w_r%d_%d" % (d, k)):
                            right(at).wait_recv()
                        to_right[at] = (part[at] + from_left[at].astype(F32)).astype(BF16)
                    else:
                        to_right[at] = part[at].astype(BF16)
                    right(at).start()

        @pl.when(z == near)
        def _():
            for d in (i, planes - 1 - i):
                if d < near:
                    at = k * planes + d
                    if h > 0:
                        with jax.named_scope("w_l%d_%d" % (d, k)):
                            left(at).wait_recv()
                        to_left[at] = (part[at] + from_right[at].astype(F32)).astype(BF16)
                    else:
                        to_left[at] = part[at].astype(BF16)
                    left(at).start()

    other = pl.ds(pl.multiple_of((1 - x) * share, 64), share)
    own = pl.ds(pl.multiple_of(x * share, 64), share)
    swaps = [
        copy(swap_out.at[k], swap_in.at[k], s_send.at[k], s_recv.at[k], xn)
        for k in range(CHUNKS)
    ]

    def finish(k):
        at = k * planes + z

        @pl.when(z > 0)
        def _():
            with jax.named_scope("w_fr%d" % k):
                right(at).wait_recv()
            part[at] += from_left[at].astype(F32)

        @pl.when(z < planes - 1)
        def _():
            with jax.named_scope("w_fl%d" % k):
                left(at).wait_recv()
            part[at] += from_right[at].astype(F32)

        swap_out[k] = part[at, other, :].astype(BF16)
        swaps[k].start()
        for side in range(2):
            @pl.when(x == side)
            def _():
                lo = side * half + k * part_cols
                out_ref[:, lo:lo + part_cols] = part[at, own, :]

    def settle(k):
        with jax.named_scope("w_swap%d" % k):
            swaps[k].wait_recv()
        for side in range(2):
            @pl.when(x == side)
            def _():
                lo = (1 - side) * half + k * part_cols
                out_ref[:, lo:lo + part_cols] = swap_in[k].astype(F32)

    gain_zs = [
        copy(gain_sum, gain_z.at[step], g_send.at[2 + step], g_recv.at[2 + step], z_peers[step])
        for step in range(planes - 1)
    ]
    reach = {}

    def begin(i, k):
        products(i, k)
        reach[i, k] = 1
        stage(0, i, k)

    def advance(i, k):
        if reach[i, k] <= planes - 2 - i:
            stage(reach[i, k], i, k)
            reach[i, k] += 1

    begin(0, 0)
    for b in order[2:]:
        forward_a(b)
    for k in range(2, CHUNKS):
        ux[k].start()
        uy[k].start()
    forward_u(1)
    advance(0, 0)
    begin(0, 1)
    advance(0, 0)
    for i in range(1, pairs):
        begin(i, 0)
        begin(i, 1)
    advance(0, 1)
    forward_u(2)
    arrive("gain_x", gain_x)
    gain_mid[...] = gain_own[...] + gain_in[0]
    gain_y.start()
    for i in range(1, pairs):
        advance(i, 0)
    advance(0, 1)
    for i in range(1, pairs):
        advance(i, 1)
    for k in range(2, CHUNKS):
        if k + 1 < CHUNKS:
            forward_u(k + 1)
        for i in range(pairs):
            begin(i, k)
        if k + 1 < CHUNKS:
            for i in range(pairs):
                advance(i, k)
        if k == 2:
            arrive("gain_y", gain_y)
            gain_sum[...] = gain_mid[...] + gain_in[1]
            for tiny in gain_zs:
                tiny.start()
    finish(0)
    done = 1
    while any(reach[i, k] <= planes - 2 - i for i, k in reach):
        for i, k in block_order(planes, CHUNKS):
            advance(i, k)
        if done < CHUNKS - 2:
            finish(done)
            settle(done - 1)
            done += 1
    for k in range(done, CHUNKS):
        finish(k)
        settle(k - 1)
    with jax.named_scope("w_gain"):
        for tiny in gain_zs:
            tiny.wait_recv()
    total_gain = gain_sum[...]
    for step in range(planes - 1):
        total_gain = total_gain + gain_z[step]
    gain_z[0] = total_gain
    for r in range(total):
        @pl.when(me == r)
        def _():
            gain_out[...] = gain_z[0, :, r * (channels // total):(r + 1) * (channels // total)]
    settle(CHUNKS - 1)

    for sent in [gain_x, gain_y] + ux + uy + ud + ax + ay + ad + swaps + gain_zs:
        sent.wait_send()
    for k in range(CHUNKS):
        for d in range(planes):
            @pl.when(d > z)
            def _():
                right(k * planes + d).wait_send()

            @pl.when(d < z)
            def _():
                left(k * planes + d).wait_send()

    @pl.when(sec > 0)
    def _():
        for mb in range(micro):
            relay(mb).wait_send()


def store_kernel(*refs):
    count = (len(refs) - 1) // 2
    sems = refs[-1]
    copies = [
        pltpu.make_async_copy(refs[n], refs[count + n], sems.at[n]) for n in range(count)
    ]
    for one in copies:
        one.start()
    for one in copies:
        one.wait()


def body(section_inputs, mix_weight, norm_gain, out_cotangent, positions):
    sections = lax.axis_size("section")
    micro, tok_mb, channels = section_inputs.shape[1:]
    tokens = micro * tok_mb
    count = lax.axis_size("dp")
    planes = count // 4
    share = channels // count
    half = channels // 2
    rows = half // planes
    vmem = pl.BlockSpec(memory_space=pltpu.VMEM)
    hbm = pl.BlockSpec(memory_space=pltpu.HBM)
    part_cols = half // CHUNKS
    hops = CHUNKS * planes
    block = (hops, rows, part_cols)
    line = (1, channels)
    sems = pltpu.SemaphoreType.DMA
    results = pl.pallas_call(
        functools.partial(back_kernel, planes, sections),
        out_shape=(
            jax.ShapeDtypeStruct((share, channels), F32),
            jax.ShapeDtypeStruct((1, share), F32),
            jax.ShapeDtypeStruct((tokens, channels), BF16),
        ),
        in_specs=[hbm] * 5,
        out_specs=(vmem, vmem, vmem),
        scratch_shapes=[
            pltpu.VMEM((tokens, channels), BF16),
            pltpu.VMEM((channels, channels), BF16),
            pltpu.VMEM((tokens, channels), BF16),
            pltpu.VMEM(line, F32),
            pltpu.VMEM((micro, tok_mb), jnp.int32),
            pltpu.VMEM((tokens, channels), F32),
            pltpu.VMEM((2, tokens, rows), BF16),
            pltpu.VMEM((rows, rows), BF16),
            pltpu.VMEM((2, half, tokens), BF16),
            pltpu.VMEM((2 * CHUNKS, tokens, part_cols), BF16),
            pltpu.VMEM((tokens, 128), F32),
            pltpu.VMEM((tokens, 128), F32),
            pltpu.VMEM((tokens, 128), F32),
            pltpu.VMEM((3, half, tokens), BF16),
            pltpu.VMEM((3 * CHUNKS, tokens, part_cols), BF16),
            pltpu.VMEM(block, F32),
            pltpu.VMEM(block, BF16),
            pltpu.VMEM(block, BF16),
            pltpu.VMEM(block, BF16),
            pltpu.VMEM(block, BF16),
            pltpu.VMEM((CHUNKS, share, part_cols), BF16),
            pltpu.VMEM((CHUNKS, share, part_cols), BF16),
            pltpu.VMEM(line, F32),
            pltpu.VMEM((2,) + line, F32),
            pltpu.VMEM(line, F32),
            pltpu.VMEM(line, F32),
            pltpu.VMEM((planes - 1,) + line, F32),
            sems((5,)), sems((micro,)), sems((micro,)),
            sems((3 * CHUNKS,)), sems((3 * CHUNKS,)), sems((3 * planes,)), sems((3 * planes,)),
            sems((CHUNKS,)), sems((CHUNKS,)), sems((hops,)), sems((hops,)),
            sems((hops,)), sems((hops,)), sems((planes + 1,)), sems((planes + 1,)),
        ],
        compiler_params=pltpu.CompilerParams(
            collective_id=0, has_side_effects=True, vmem_limit_bytes=60 << 20
        ),
    )(
        section_inputs.reshape(tokens, channels),
        mix_weight[0],
        out_cotangent.reshape(tokens, channels),
        norm_gain,
        positions,
    )
    weight_grad, gain_share, grads = pl.pallas_call(
        store_kernel,
        out_shape=tuple(jax.ShapeDtypeStruct(r.shape, r.dtype) for r in results),
        in_specs=[vmem] * 3,
        out_specs=(hbm,) * 3,
        scratch_shapes=[sems((3,))],
    )(*results)
    return (grads.reshape(1, micro, tok_mb, channels), weight_grad[None], gain_share)


def solution(mesh):
    return jax.shard_map(
        body,
        mesh=mesh,
        in_specs=(
            P("section", None, "dp", None),
            P("section", None, None),
            P("section", None),
            P(None, "dp", None),
            P(None, "dp"),
        ),
        out_specs=(P("section", None, "dp", None), P("section", "dp", None), P("section", "dp")),
        check_vma=False,
    )
```

```python
import functools
import math

import jax
import jax.numpy as jnp
from jax import lax
from jax.experimental import pallas as pl
from jax.experimental.pallas import tpu as pltpu
from jax.sharding import PartitionSpec as P

DEPTH = 1024
MESH = pl.DeviceIdType.MESH
F32 = jnp.float32
BF16 = jnp.bfloat16
ROOT = math.sqrt(2.0 / math.pi)
CUBE = 0.044715
CHUNKS = 4
GRANT = 52736


def contract(a, b, dims):
    return lax.dot_general(a, b, (dims, ((), ())), preferred_element_type=F32)


def block_order(planes, chunks):
    pairs = planes // 2
    return [(i, k + n) for k in range(0, chunks, 2) for i in range(pairs) for n in range(2)]


def back_kernel(
    planes, sections, x_hbm, w_hbm, cot_hbm, gain_hbm, pos_hbm, out_ref, gain_out, grads_ref,
    x_ref, w_ref, g_ref, gain_ref, pos_ref, slope, tmp, eye_ref, act_ref, up_ref, q_ref, m_ref,
    proj, gath_a, gath_u, part, from_left, from_right, to_right, to_left, swap_out, swap_in,
    gain_own, gain_in, gain_mid, gain_sum, gain_z,
    in_sem, sec_send, sec_recv, u_send, u_recv, a_send, a_recv, s_send, s_recv,
    r_send, r_recv, l_send, l_recv, g_send, g_recv,
):
    me = lax.axis_index("dp")
    sec = lax.axis_index("section")
    last = sections - 1
    total = planes * 4
    x = lax.rem(me, 2)
    y = lax.rem(me // 2, 2)
    z = me // 4
    xn = me + 1 - 2 * x
    yn = me + 2 - 4 * y
    tokens, channels = x_ref.shape
    half = channels // 2
    rows = half // planes
    share = rows // 2
    micro, tok_mb = pos_ref.shape
    step_rows = 16
    width = min(256, channels)
    part_cols = half // CHUNKS
    pairs = planes // 2

    load_x = pltpu.make_async_copy(x_hbm, x_ref, in_sem.at[0])
    load_w = pltpu.make_async_copy(w_hbm, w_ref, in_sem.at[1])
    load_g = pltpu.make_async_copy(cot_hbm, g_ref, in_sem.at[2])
    load_gain = pltpu.make_async_copy(gain_hbm, gain_ref, in_sem.at[3])
    load_pos = pltpu.make_async_copy(pos_hbm, pos_ref, in_sem.at[4])
    load_pos.start()

    @pl.when(sec == last)
    def _():
        load_g.start()

    load_x.start()
    load_gain.start()
    load_w.start()

    def copy(src, dst, send, recv, to):
        return pltpu.make_async_remote_copy(
            src_ref=src, dst_ref=dst, send_sem=send, recv_sem=recv,
            device_id={"dp": to}, device_id_type=MESH,
        )

    barrier = pltpu.get_barrier_semaphore()
    z_peers = [lax.rem(me + 4 * step, total) for step in range(1, planes)]
    for peer in [xn, yn] + z_peers:
        pl.semaphore_signal(barrier, inc=1, device_id={"dp": peer}, device_id_type=MESH)

    @pl.when(sec > 0)
    def _():
        pl.semaphore_signal(barrier, inc=1, device_id={"section": sec - 1}, device_id_type=MESH)

    @pl.when(sec < last)
    def _():
        pl.semaphore_signal(barrier, inc=1, device_id={"section": sec + 1}, device_id_type=MESH)

    proj[...] = jnp.zeros_like(proj)
    at_row = lax.broadcasted_iota(jnp.int32, (rows, rows), 0)
    at_col = lax.broadcasted_iota(jnp.int32, (rows, rows), 1)
    eye_ref[...] = jnp.where(at_row == at_col, 1.0, 0.0).astype(BF16)
    with jax.named_scope("w_pos"):
        load_pos.wait()
    factor = 1.0 + 0.5 * jnp.sin(2.0 * math.pi * pos_ref[...].astype(F32) / DEPTH)
    for mb in range(micro):
        m_ref[mb * tok_mb:(mb + 1) * tok_mb, :] = jnp.transpose(
            jnp.broadcast_to(factor[mb:mb + 1, :], (128, tok_mb))
        )

    ux = [
        copy(up_ref.at[(1 - x) * CHUNKS + k], gath_u.at[k], u_send.at[k], u_recv.at[k], xn)
        for k in range(CHUNKS)
    ]
    uy = [
        copy(
            up_ref.at[x * CHUNKS + k], gath_u.at[CHUNKS + k],
            u_send.at[CHUNKS + k], u_recv.at[CHUNKS + k], yn,
        )
        for k in range(CHUNKS)
    ]
    ud = [
        copy(
            gath_u.at[k], gath_u.at[2 * CHUNKS + k],
            u_send.at[2 * CHUNKS + k], u_recv.at[2 * CHUNKS + k], yn,
        )
        for k in range(CHUNKS)
    ]
    spans = [pl.ds(b * rows, rows) for b in range(planes)]
    ax = [
        copy(act_ref.at[y, spans[b]], gath_a.at[0, spans[b]], a_send.at[b], a_recv.at[b], xn)
        for b in range(planes)
    ]
    ay = [
        copy(
            act_ref.at[1 - y, spans[b]], gath_a.at[1, spans[b]],
            a_send.at[planes + b], a_recv.at[planes + b], yn,
        )
        for b in range(planes)
    ]
    ad = [
        copy(
            gath_a.at[1, spans[b]], gath_a.at[2, spans[b]],
            a_send.at[2 * planes + b], a_recv.at[2 * planes + b], xn,
        )
        for b in range(planes)
    ]
    gain_x = copy(gain_own, gain_in.at[0], g_send.at[0], g_recv.at[0], xn)
    gain_y = copy(gain_mid, gain_in.at[1], g_send.at[1], g_recv.at[1], yn)

    def relay(mb):
        span = pl.ds(mb * tok_mb, tok_mb)
        return pltpu.make_async_remote_copy(
            src_ref=grads_ref.at[span, :], dst_ref=g_ref.at[span, :],
            send_sem=sec_send.at[mb], recv_sem=sec_recv.at[mb],
            device_id={"section": jnp.maximum(sec - 1, 0)}, device_id_type=MESH,
        )

    arrived = set()

    def arrive(name, sent, again=False):
        if again or name not in arrived:
            arrived.add(name)
            with jax.named_scope("w_" + name):
                sent.wait_recv()

    def forward_u(k):
        arrive("ux%d" % k, ux[k], True)
        ud[k].start()

    def forward_a(b):
        arrive("ay%d" % b, ay[b], True)
        ad[b].start()

    def upstream(mb):
        @pl.loop(mb * (tok_mb // step_rows), (mb + 1) * (tok_mb // step_rows))
        def _(i):
            r = pl.ds(pl.multiple_of(i * step_rows, step_rows), step_rows)
            m = m_ref[r, :]
            for c in range(channels // 128):
                at = c * 128
                g = g_ref[r, at:at + 128].astype(F32)
                low = at % part_cols
                up_ref[at // part_cols, r, low:low + 128] = (m * g).astype(BF16)

    @pl.when(sec == last)
    def _():
        with jax.named_scope("w_g"):
            load_g.wait()
        for mb in range(micro):
            upstream(mb)

    beside = jnp.minimum(sec, 1) + jnp.minimum(last - sec, 1)
    with jax.named_scope("barrier"):
        pl.semaphore_wait(barrier, 1 + planes + beside)

    @pl.when(sec == last)
    def _():
        ux[0].start()
        uy[0].start()

    with jax.named_scope("w_x"):
        load_x.wait()
        load_gain.wait()

    @pl.loop(0, tokens // step_rows)
    def _(i):
        r = pl.ds(pl.multiple_of(i * step_rows, step_rows), step_rows)
        square = jnp.zeros((step_rows, rows), F32)
        for c in range(channels // rows):
            xc = x_ref[r, c * rows:(c + 1) * rows].astype(F32)
            square = square + xc * xc
        q = lax.rsqrt(jnp.sum(square, axis=-1, keepdims=True) / channels + 1e-06)
        q_ref[r, :] = jnp.broadcast_to(q, (step_rows, 128))

    tall = 32

    def activate(b):
        @pl.loop(0, tokens // tall)
        def _(i):
            r = pl.ds(pl.multiple_of(i * tall, tall), tall)
            q = q_ref[r, :]
            for c in range(2 * rows // 128):
                at = 2 * b * rows + c * 128
                cols = slice(at, at + 128)
                low = c * 128 % rows
                n = x_ref[r, cols].astype(F32) * q * gain_ref[:, cols]
                n2 = n * n
                th = jnp.tanh(n * (ROOT + (ROOT * CUBE) * n2))
                cdf = 0.5 + 0.5 * th
                tmp[c * 128 // rows, r, low:low + 128] = (n * cdf).astype(BF16)
                bend = n * (0.5 * ROOT + (1.5 * ROOT * CUBE) * n2)
                slope[r, cols] = cdf + bend * (1.0 - th * th)

        for side in range(2):
            act_ref[side, spans[b], :] = contract(eye_ref[...], tmp[side], ((1,), (1,))).astype(BF16)

    order = []
    for i in range(pairs):
        order += [i, planes - 1 - i]
    for n, b in enumerate(order):
        activate(b)
        if n < 2:
            @pl.when(sec == last)
            def _():
                ay[b].start()
                ax[b].start()

    @pl.when(sec < last)
    def _():
        for mb in range(micro):
            with jax.named_scope("w_relay%d" % mb):
                relay(mb).wait_recv()
            upstream(mb)
        ux[0].start()
        uy[0].start()
        for b in order[:2]:
            ay[b].start()
            ax[b].start()

    @pl.when(sec == last)
    def _():
        forward_u(0)

    with jax.named_scope("w_w"):
        load_w.wait()

    def back_columns(start, stop):
        @pl.loop(start, stop)
        def _(c):
            cols = pl.ds(pl.multiple_of(c * width, width), width)
            back = jnp.zeros((tokens, width), F32)
            for h in range(2 * CHUNKS):
                back = back + contract(
                    up_ref[h], w_ref[cols, h * part_cols:(h + 1) * part_cols], ((1,), (1,))
                )
            lanes = proj[...]
            q = q_ref[...]
            for k in range(width // 128):
                piece = pl.ds(pl.multiple_of(c * width + k * 128, 128), 128)
                grad_norm = back[:, k * 128:(k + 1) * 128] * slope[:, piece]
                xc = x_ref[:, piece].astype(F32)
                scaled = grad_norm * gain_ref[:, piece]
                slope[:, piece] = scaled
                lanes = lanes + scaled * xc
                gain_own[:, piece] = jnp.sum(grad_norm * xc * q, axis=0, keepdims=True)
            proj[...] = lanes

    def send_rest():
        for b in order[2:]:
            ay[b].start()
            ax[b].start()

    steps = channels // width
    back_columns(0, steps // 4)

    @pl.when(sec == last)
    def _():
        forward_a(order[0])

    back_columns(steps // 4, steps // 2)

    @pl.when(sec == last)
    def _():
        forward_a(order[1])
        ux[1].start()
        send_rest()
        uy[1].start()

    back_columns(steps // 2, steps)
    gain_x.start()

    for mb in range(micro):
        @pl.loop(mb * (tok_mb // step_rows), (mb + 1) * (tok_mb // step_rows))
        def _(i):
            r = pl.ds(pl.multiple_of(i * step_rows, step_rows), step_rows)
            q = q_ref[r, :]
            along = jnp.sum(proj[r, :], axis=-1, keepdims=True) / channels
            pull = (q * q * q) * jnp.broadcast_to(along, (step_rows, 128))
            for c in range(channels // 128):
                cols = slice(c * 128, (c + 1) * 128)
                delta = q * slope[r, cols] - x_ref[r, cols].astype(F32) * pull
                grads_ref[r, cols] = (g_ref[r, cols].astype(F32) + delta).astype(BF16)

        @pl.when(sec > 0)
        def _():
            relay(mb).start()

    @pl.when(sec < last)
    def _():
        forward_u(0)
        ux[1].start()
        uy[1].start()
        for b in order[:2]:
            forward_a(b)
        send_rest()

    z_next = lax.rem(me + 4, total)
    z_prev = lax.rem(me + total - 4, total)

    def right(at):
        return copy(to_right.at[at], from_left.at[at], r_send.at[at], r_recv.at[at], z_next)

    def left(at):
        return copy(to_left.at[at], from_right.at[at], l_send.at[at], l_recv.at[at], z_prev)

    def products(i, k):
        for b in (i, planes - 1 - i):
            arrive("ax%d" % b, ax[b])
            arrive("ad%d" % b, ad[b])
        arrive("uy%d" % k, uy[k])
        arrive("ud%d" % k, ud[k])

        @pl.loop(0, 2)
        def _(n):
            b = i + n * (planes - 1 - 2 * i)
            span = pl.ds(pl.multiple_of(b * rows, rows), rows)
            inner = ((1,), (0,))
            term = contract(act_ref[y, span, :], up_ref[x * CHUNKS + k], inner)
            for slot in range(3):
                term = term + contract(
                    gath_a[slot, span, :], gath_u[slot * CHUNKS + k], inner
                )
            part[k * planes + b] = term

    def stage(h, i, k):
        near = planes - 1 - h

        @pl.when(z == h)
        def _():
            for d in (planes - 1 - i, i):
                if d > h:
                    at = k * planes + d
                    if h > 0:
                        with jax.named_scope("w_r%d_%d" % (d, k)):
                            right(at).wait_recv()
                        to_right[at] = (part[at] + from_left[at].astype(F32)).astype(BF16)
                    else:
                        to_right[at] = part[at].astype(BF16)
                    right(at).start()

        @pl.when(z == near)
        def _():
            for d in (i, planes - 1 - i):
                if d < near:
                    at = k * planes + d
                    if h > 0:
                        with jax.named_scope("w_l%d_%d" % (d, k)):
                            left(at).wait_recv()
                        to_left[at] = (part[at] + from_right[at].astype(F32)).astype(BF16)
                    else:
                        to_left[at] = part[at].astype(BF16)
                    left(at).start()

    other = pl.ds(pl.multiple_of((1 - x) * share, 64), share)
    own = pl.ds(pl.multiple_of(x * share, 64), share)
    swaps = [
        copy(swap_out.at[k], swap_in.at[k], s_send.at[k], s_recv.at[k], xn)
        for k in range(CHUNKS)
    ]

    def finish(k):
        at = k * planes + z

        @pl.when(z > 0)
        def _():
            with jax.named_scope("w_fr%d" % k):
                right(at).wait_recv()
            part[at] += from_left[at].astype(F32)

        @pl.when(z < planes - 1)
        def _():
            with jax.named_scope("w_fl%d" % k):
                left(at).wait_recv()
            part[at] += from_right[at].astype(F32)

        swap_out[k] = part[at, other, :].astype(BF16)
        swaps[k].start()
        for side in range(2):
            @pl.when(x == side)
            def _():
                lo = side * half + k * part_cols
                out_ref[:, lo:lo + part_cols] = part[at, own, :]

    def settle(k):
        with jax.named_scope("w_swap%d" % k):
            swaps[k].wait_recv()
        for side in range(2):
            @pl.when(x == side)
            def _():
                lo = (1 - side) * half + k * part_cols
                out_ref[:, lo:lo + part_cols] = swap_in[k].astype(F32)

    gain_zs = [
        copy(gain_sum, gain_z.at[step], g_send.at[2 + step], g_recv.at[2 + step], z_peers[step])
        for step in range(planes - 1)
    ]
    reach = {}

    def begin(i, k):
        products(i, k)
        reach[i, k] = 1
        stage(0, i, k)

    def advance(i, k):
        if reach[i, k] <= planes - 2 - i:
            stage(reach[i, k], i, k)
            reach[i, k] += 1

    begin(0, 0)
    forward_u(1)
    for b in order[2:]:
        forward_a(b)
    for k in range(2, CHUNKS):
        ux[k].start()
        uy[k].start()
    advance(0, 0)
    begin(0, 1)
    advance(0, 0)
    for i in range(1, pairs):
        begin(i, 0)
        begin(i, 1)
    advance(0, 1)
    for k in range(2, CHUNKS):
        forward_u(k)
    arrive("gain_x", gain_x)
    gain_mid[...] = gain_own[...] + gain_in[0]
    gain_y.start()
    for i in range(1, pairs):
        advance(i, 0)
    advance(0, 1)
    for i in range(1, pairs):
        advance(i, 1)
    for k in range(2, CHUNKS, 2):
        begin(0, k)
        begin(0, k + 1)
        advance(0, k)
        for i in range(1, pairs):
            begin(i, k)
        advance(0, k + 1)
        for i in range(1, pairs):
            begin(i, k + 1)
        if k == 2:
            arrive("gain_y", gain_y)
            gain_sum[...] = gain_mid[...] + gain_in[1]
            for tiny in gain_zs:
                tiny.start()
    finish(0)
    done = 1
    while any(reach[i, k] <= planes - 2 - i for i, k in reach):
        for i, k in block_order(planes, CHUNKS):
            advance(i, k)
        if done < CHUNKS - 2:
            finish(done)
            settle(done - 1)
            done += 1
    for k in range(done, CHUNKS):
        finish(k)
        settle(k - 1)
    with jax.named_scope("w_gain"):
        for tiny in gain_zs:
            tiny.wait_recv()
    total_gain = gain_sum[...]
    for step in range(planes - 1):
        total_gain = total_gain + gain_z[step]
    gain_z[0] = total_gain
    for r in range(total):
        @pl.when(me == r)
        def _():
            gain_out[...] = gain_z[0, :, r * (channels // total):(r + 1) * (channels // total)]
    settle(CHUNKS - 1)

    for sent in [gain_x, gain_y] + ux + uy + ud + ax + ay + ad + swaps + gain_zs:
        sent.wait_send()
    for k in range(CHUNKS):
        for d in range(planes):
            @pl.when(d > z)
            def _():
                right(k * planes + d).wait_send()

            @pl.when(d < z)
            def _():
                left(k * planes + d).wait_send()

    @pl.when(sec > 0)
    def _():
        for mb in range(micro):
            relay(mb).wait_send()


def store_kernel(*refs):
    count = (len(refs) - 1) // 2
    sems = refs[-1]
    copies = [
        pltpu.make_async_copy(refs[n], refs[count + n], sems.at[n]) for n in range(count)
    ]
    for one in copies:
        one.start()
    for one in copies:
        one.wait()


def body(section_inputs, mix_weight, norm_gain, out_cotangent, positions):
    sections = lax.axis_size("section")
    micro, tok_mb, channels = section_inputs.shape[1:]
    tokens = micro * tok_mb
    count = lax.axis_size("dp")
    planes = count // 4
    share = channels // count
    half = channels // 2
    rows = half // planes
    vmem = pl.BlockSpec(memory_space=pltpu.VMEM)
    hbm = pl.BlockSpec(memory_space=pltpu.HBM)
    part_cols = half // CHUNKS
    hops = CHUNKS * planes
    block = (hops, rows, part_cols)
    line = (1, channels)
    sems = pltpu.SemaphoreType.DMA
    results = pl.pallas_call(
        functools.partial(back_kernel, planes, sections),
        out_shape=(
            jax.ShapeDtypeStruct((share, channels), F32),
            jax.ShapeDtypeStruct((1, share), F32),
            jax.ShapeDtypeStruct((tokens, channels), BF16),
        ),
        in_specs=[hbm] * 5,
        out_specs=(vmem, vmem, vmem),
        scratch_shapes=[
            pltpu.VMEM((tokens, channels), BF16),
            pltpu.VMEM((channels, channels), BF16),
            pltpu.VMEM((tokens, channels), BF16),
            pltpu.VMEM(line, F32),
            pltpu.VMEM((micro, tok_mb), jnp.int32),
            pltpu.VMEM((tokens, channels), F32),
            pltpu.VMEM((2, tokens, rows), BF16),
            pltpu.VMEM((rows, rows), BF16),
            pltpu.VMEM((2, half, tokens), BF16),
            pltpu.VMEM((2 * CHUNKS, tokens, part_cols), BF16),
            pltpu.VMEM((tokens, 128), F32),
            pltpu.VMEM((tokens, 128), F32),
            pltpu.VMEM((tokens, 128), F32),
            pltpu.VMEM((3, half, tokens), BF16),
            pltpu.VMEM((3 * CHUNKS, tokens, part_cols), BF16),
            pltpu.VMEM(block, F32),
            pltpu.VMEM(block, BF16),
            pltpu.VMEM(block, BF16),
            pltpu.VMEM(block, BF16),
            pltpu.VMEM(block, BF16),
            pltpu.VMEM((CHUNKS, share, part_cols), BF16),
            pltpu.VMEM((CHUNKS, share, part_cols), BF16),
            pltpu.VMEM(line, F32),
            pltpu.VMEM((2,) + line, F32),
            pltpu.VMEM(line, F32),
            pltpu.VMEM(line, F32),
            pltpu.VMEM((planes - 1,) + line, F32),
            sems((5,)), sems((micro,)), sems((micro,)),
            sems((3 * CHUNKS,)), sems((3 * CHUNKS,)), sems((3 * planes,)), sems((3 * planes,)),
            sems((CHUNKS,)), sems((CHUNKS,)), sems((hops,)), sems((hops,)),
            sems((hops,)), sems((hops,)), sems((planes + 1,)), sems((planes + 1,)),
        ],
        compiler_params=pltpu.CompilerParams(
            collective_id=0, has_side_effects=True, vmem_limit_bytes=GRANT << 10
        ),
    )(
        section_inputs.reshape(tokens, channels),
        mix_weight[0],
        out_cotangent.reshape(tokens, channels),
        norm_gain,
        positions,
    )
    weight_grad, gain_share, grads = pl.pallas_call(
        store_kernel,
        out_shape=tuple(jax.ShapeDtypeStruct(r.shape, r.dtype) for r in results),
        in_specs=[vmem] * 3,
        out_specs=(hbm,) * 3,
        scratch_shapes=[sems((3,))],
        compiler_params=pltpu.CompilerParams(vmem_limit_bytes=4 << 20),
    )(*results)
    return (grads.reshape(1, micro, tok_mb, channels), weight_grad[None], gain_share)


def solution(mesh):
    return jax.shard_map(
        body,
        mesh=mesh,
        in_specs=(
            P("section", None, "dp", None),
            P("section", None, None),
            P("section", None),
            P(None, "dp", None),
            P(None, "dp"),
        ),
        out_specs=(P("section", None, "dp", None), P("section", "dp", None), P("section", "dp")),
        check_vma=False,
    )
```

```python
import functools
import math

import jax
import jax.numpy as jnp
from jax import lax
from jax.experimental import pallas as pl
from jax.experimental.pallas import tpu as pltpu
from jax.sharding import PartitionSpec as P

DEPTH = 1024
MESH = pl.DeviceIdType.MESH
F32 = jnp.float32
BF16 = jnp.bfloat16
ROOT = math.sqrt(2.0 / math.pi)
CUBE = 0.044715
CHUNKS = 4
GRANT = 52736


def contract(a, b, dims):
    return lax.dot_general(a, b, (dims, ((), ())), preferred_element_type=F32)


def block_order(planes, chunks):
    pairs = planes // 2
    return [(i, k + n) for k in range(0, chunks, 2) for i in range(pairs) for n in range(2)]


def back_kernel(
    planes, sections, x_hbm, w_hbm, cot_hbm, gain_hbm, pos_hbm, out_ref, gain_out, grads_ref,
    x_ref, w_ref, g_ref, gain_ref, pos_ref, slope, tmp, eye_ref, act_ref, up_ref, q_ref, m_ref,
    proj, gath_a, gath_u, part, from_left, from_right, to_right, to_left, swap_out, swap_in,
    gain_own, gain_in, gain_mid, gain_sum, gain_z,
    in_sem, sec_send, sec_recv, u_send, u_recv, a_send, a_recv, s_send, s_recv,
    r_send, r_recv, l_send, l_recv, g_send, g_recv,
):
    me = lax.axis_index("dp")
    sec = lax.axis_index("section")
    last = sections - 1
    total = planes * 4
    x = lax.rem(me, 2)
    y = lax.rem(me // 2, 2)
    z = me // 4
    xn = me + 1 - 2 * x
    yn = me + 2 - 4 * y
    tokens, channels = x_ref.shape
    half = channels // 2
    rows = half // planes
    share = rows // 2
    micro, tok_mb = pos_ref.shape
    step_rows = 16
    width = min(256, channels)
    part_cols = half // CHUNKS
    pairs = planes // 2

    load_x = pltpu.make_async_copy(x_hbm, x_ref, in_sem.at[0])
    load_w = pltpu.make_async_copy(w_hbm, w_ref, in_sem.at[1])
    load_g = pltpu.make_async_copy(cot_hbm, g_ref, in_sem.at[2])
    load_gain = pltpu.make_async_copy(gain_hbm, gain_ref, in_sem.at[3])
    load_pos = pltpu.make_async_copy(pos_hbm, pos_ref, in_sem.at[4])
    load_pos.start()

    @pl.when(sec == last)
    def _():
        load_g.start()

    load_x.start()
    load_gain.start()
    load_w.start()

    def copy(src, dst, send, recv, to):
        return pltpu.make_async_remote_copy(
            src_ref=src, dst_ref=dst, send_sem=send, recv_sem=recv,
            device_id={"dp": to}, device_id_type=MESH,
        )

    barrier = pltpu.get_barrier_semaphore()
    z_peers = [lax.rem(me + 4 * step, total) for step in range(1, planes)]
    for peer in [xn, yn] + z_peers:
        pl.semaphore_signal(barrier, inc=1, device_id={"dp": peer}, device_id_type=MESH)

    @pl.when(sec > 0)
    def _():
        pl.semaphore_signal(barrier, inc=1, device_id={"section": sec - 1}, device_id_type=MESH)

    @pl.when(sec < last)
    def _():
        pl.semaphore_signal(barrier, inc=1, device_id={"section": sec + 1}, device_id_type=MESH)

    proj[...] = jnp.zeros_like(proj)
    at_row = lax.broadcasted_iota(jnp.int32, (rows, rows), 0)
    at_col = lax.broadcasted_iota(jnp.int32, (rows, rows), 1)
    eye_ref[...] = jnp.where(at_row == at_col, 1.0, 0.0).astype(BF16)
    with jax.named_scope("w_pos"):
        load_pos.wait()
    factor = 1.0 + 0.5 * jnp.sin(2.0 * math.pi * pos_ref[...].astype(F32) / DEPTH)
    for mb in range(micro):
        m_ref[mb * tok_mb:(mb + 1) * tok_mb, :] = jnp.transpose(
            jnp.broadcast_to(factor[mb:mb + 1, :], (128, tok_mb))
        )

    ux = [
        copy(up_ref.at[(1 - x) * CHUNKS + k], gath_u.at[k], u_send.at[k], u_recv.at[k], xn)
        for k in range(CHUNKS)
    ]
    uy = [
        copy(
            up_ref.at[x * CHUNKS + k], gath_u.at[CHUNKS + k],
            u_send.at[CHUNKS + k], u_recv.at[CHUNKS + k], yn,
        )
        for k in range(CHUNKS)
    ]
    ud = [
        copy(
            gath_u.at[k], gath_u.at[2 * CHUNKS + k],
            u_send.at[2 * CHUNKS + k], u_recv.at[2 * CHUNKS + k], yn,
        )
        for k in range(CHUNKS)
    ]
    spans = [pl.ds(b * rows, rows) for b in range(planes)]
    ax = [
        copy(act_ref.at[y, spans[b]], gath_a.at[0, spans[b]], a_send.at[b], a_recv.at[b], xn)
        for b in range(planes)
    ]
    ay = [
        copy(
            act_ref.at[1 - y, spans[b]], gath_a.at[1, spans[b]],
            a_send.at[planes + b], a_recv.at[planes + b], yn,
        )
        for b in range(planes)
    ]
    ad = [
        copy(
            gath_a.at[1, spans[b]], gath_a.at[2, spans[b]],
            a_send.at[2 * planes + b], a_recv.at[2 * planes + b], xn,
        )
        for b in range(planes)
    ]
    gain_x = copy(gain_own, gain_in.at[0], g_send.at[0], g_recv.at[0], xn)
    gain_y = copy(gain_mid, gain_in.at[1], g_send.at[1], g_recv.at[1], yn)

    def relay(mb):
        span = pl.ds(mb * tok_mb, tok_mb)
        return pltpu.make_async_remote_copy(
            src_ref=grads_ref.at[span, :], dst_ref=g_ref.at[span, :],
            send_sem=sec_send.at[mb], recv_sem=sec_recv.at[mb],
            device_id={"section": jnp.maximum(sec - 1, 0)}, device_id_type=MESH,
        )

    arrived = set()

    def arrive(name, sent, again=False):
        if again or name not in arrived:
            arrived.add(name)
            with jax.named_scope("w_" + name):
                sent.wait_recv()

    def forward_u(k):
        arrive("ux%d" % k, ux[k], True)
        ud[k].start()

    def forward_a(b):
        arrive("ay%d" % b, ay[b], True)
        ad[b].start()

    def upstream(mb):
        @pl.loop(mb * (tok_mb // step_rows), (mb + 1) * (tok_mb // step_rows))
        def _(i):
            r = pl.ds(pl.multiple_of(i * step_rows, step_rows), step_rows)
            m = m_ref[r, :]
            for c in range(channels // 128):
                at = c * 128
                g = g_ref[r, at:at + 128].astype(F32)
                low = at % part_cols
                up_ref[at // part_cols, r, low:low + 128] = (m * g).astype(BF16)

    @pl.when(sec == last)
    def _():
        with jax.named_scope("w_g"):
            load_g.wait()
        for mb in range(micro):
            upstream(mb)

    beside = jnp.minimum(sec, 1) + jnp.minimum(last - sec, 1)
    with jax.named_scope("barrier"):
        pl.semaphore_wait(barrier, 1 + planes + beside)

    @pl.when(sec == last)
    def _():
        ux[0].start()
        uy[0].start()

    with jax.named_scope("w_x"):
        load_x.wait()
        load_gain.wait()

    @pl.loop(0, tokens // step_rows)
    def _(i):
        r = pl.ds(pl.multiple_of(i * step_rows, step_rows), step_rows)
        square = jnp.zeros((step_rows, rows), F32)
        for c in range(channels // rows):
            xc = x_ref[r, c * rows:(c + 1) * rows].astype(F32)
            square = square + xc * xc
        q = lax.rsqrt(jnp.sum(square, axis=-1, keepdims=True) / channels + 1e-06)
        q_ref[r, :] = jnp.broadcast_to(q, (step_rows, 128))

    tall = 32

    def activate(b):
        @pl.loop(0, tokens // tall)
        def _(i):
            r = pl.ds(pl.multiple_of(i * tall, tall), tall)
            q = q_ref[r, :]
            for c in range(2 * rows // 128):
                at = 2 * b * rows + c * 128
                cols = slice(at, at + 128)
                low = c * 128 % rows
                n = x_ref[r, cols].astype(F32) * q * gain_ref[:, cols]
                n2 = n * n
                th = jnp.tanh(n * (ROOT + (ROOT * CUBE) * n2))
                cdf = 0.5 + 0.5 * th
                tmp[c * 128 // rows, r, low:low + 128] = (n * cdf).astype(BF16)
                bend = n * (0.5 * ROOT + (1.5 * ROOT * CUBE) * n2)
                slope[r, cols] = cdf + bend * (1.0 - th * th)

        for side in range(2):
            act_ref[side, spans[b], :] = contract(eye_ref[...], tmp[side], ((1,), (1,))).astype(BF16)

    order = []
    for i in range(pairs):
        order += [i, planes - 1 - i]
    for n, b in enumerate(order):
        activate(b)
        if n < 2:
            @pl.when(sec == last)
            def _():
                ay[b].start()
                ax[b].start()

    @pl.when(sec < last)
    def _():
        for mb in range(micro):
            with jax.named_scope("w_relay%d" % mb):
                relay(mb).wait_recv()
            upstream(mb)

    @pl.when(sec == last)
    def _():
        forward_u(0)
        ux[1].start()
        uy[1].start()

    with jax.named_scope("w_w"):
        load_w.wait()

    def back_columns(start, stop):
        @pl.loop(start, stop)
        def _(c):
            cols = pl.ds(pl.multiple_of(c * width, width), width)
            back = jnp.zeros((tokens, width), F32)
            for h in range(2 * CHUNKS):
                back = back + contract(
                    up_ref[h], w_ref[cols, h * part_cols:(h + 1) * part_cols], ((1,), (1,))
                )
            lanes = proj[...]
            q = q_ref[...]
            for k in range(width // 128):
                piece = pl.ds(pl.multiple_of(c * width + k * 128, 128), 128)
                grad_norm = back[:, k * 128:(k + 1) * 128] * slope[:, piece]
                xc = x_ref[:, piece].astype(F32)
                scaled = grad_norm * gain_ref[:, piece]
                slope[:, piece] = scaled
                lanes = lanes + scaled * xc
                gain_own[:, piece] = jnp.sum(grad_norm * xc * q, axis=0, keepdims=True)
            proj[...] = lanes

    def send_rest():
        for b in order[2:]:
            ay[b].start()
            ax[b].start()

    steps = channels // width
    back_columns(0, steps // 4)

    @pl.when(sec == last)
    def _():
        forward_a(order[0])

    back_columns(steps // 4, steps // 2)

    @pl.when(sec == last)
    def _():
        forward_a(order[1])
        send_rest()

    @pl.when(sec < last)
    def _():
        ux[0].start()
        uy[0].start()
        for b in order[:2]:
            ay[b].start()
            ax[b].start()

    back_columns(steps // 2, steps)
    gain_x.start()

    @pl.when(sec == last)
    def _():
        forward_u(1)

    for mb in range(micro):
        @pl.loop(mb * (tok_mb // step_rows), (mb + 1) * (tok_mb // step_rows))
        def _(i):
            r = pl.ds(pl.multiple_of(i * step_rows, step_rows), step_rows)
            q = q_ref[r, :]
            along = jnp.sum(proj[r, :], axis=-1, keepdims=True) / channels
            pull = (q * q * q) * jnp.broadcast_to(along, (step_rows, 128))
            for c in range(channels // 128):
                cols = slice(c * 128, (c + 1) * 128)
                delta = q * slope[r, cols] - x_ref[r, cols].astype(F32) * pull
                grads_ref[r, cols] = (g_ref[r, cols].astype(F32) + delta).astype(BF16)

        @pl.when(sec > 0)
        def _():
            relay(mb).start()

    @pl.when(sec < last)
    def _():
        forward_u(0)
        ux[1].start()
        uy[1].start()
        for b in order[:2]:
            forward_a(b)
        send_rest()
        forward_u(1)
        for b in order[2:]:
            forward_a(b)

    z_next = lax.rem(me + 4, total)
    z_prev = lax.rem(me + total - 4, total)

    def right(at):
        return copy(to_right.at[at], from_left.at[at], r_send.at[at], r_recv.at[at], z_next)

    def left(at):
        return copy(to_left.at[at], from_right.at[at], l_send.at[at], l_recv.at[at], z_prev)

    def products(i, k):
        for b in (i, planes - 1 - i):
            arrive("ax%d" % b, ax[b])
            arrive("ad%d" % b, ad[b])
        arrive("uy%d" % k, uy[k])
        arrive("ud%d" % k, ud[k])

        @pl.loop(0, 2)
        def _(n):
            b = i + n * (planes - 1 - 2 * i)
            span = pl.ds(pl.multiple_of(b * rows, rows), rows)
            inner = ((1,), (0,))
            term = contract(act_ref[y, span, :], up_ref[x * CHUNKS + k], inner)
            for slot in range(3):
                term = term + contract(
                    gath_a[slot, span, :], gath_u[slot * CHUNKS + k], inner
                )
            part[k * planes + b] = term

    def stage(h, i, k):
        near = planes - 1 - h

        @pl.when(z == h)
        def _():
            for d in (planes - 1 - i, i):
                if d > h:
                    at = k * planes + d
                    if h > 0:
                        with jax.named_scope("w_r%d_%d" % (d, k)):
                            right(at).wait_recv()
                        to_right[at] = (part[at] + from_left[at].astype(F32)).astype(BF16)
                    else:
                        to_right[at] = part[at].astype(BF16)
                    right(at).start()

        @pl.when(z == near)
        def _():
            for d in (i, planes - 1 - i):
                if d < near:
                    at = k * planes + d
                    if h > 0:
                        with jax.named_scope("w_l%d_%d" % (d, k)):
                            left(at).wait_recv()
                        to_left[at] = (part[at] + from_right[at].astype(F32)).astype(BF16)
                    else:
                        to_left[at] = part[at].astype(BF16)
                    left(at).start()

    other = pl.ds(pl.multiple_of((1 - x) * share, 64), share)
    own = pl.ds(pl.multiple_of(x * share, 64), share)
    swaps = [
        copy(swap_out.at[k], swap_in.at[k], s_send.at[k], s_recv.at[k], xn)
        for k in range(CHUNKS)
    ]

    def finish(k):
        at = k * planes + z

        @pl.when(z > 0)
        def _():
            with jax.named_scope("w_fr%d" % k):
                right(at).wait_recv()
            part[at] += from_left[at].astype(F32)

        @pl.when(z < planes - 1)
        def _():
            with jax.named_scope("w_fl%d" % k):
                left(at).wait_recv()
            part[at] += from_right[at].astype(F32)

        swap_out[k] = part[at, other, :].astype(BF16)
        swaps[k].start()
        for side in range(2):
            @pl.when(x == side)
            def _():
                lo = side * half + k * part_cols
                out_ref[:, lo:lo + part_cols] = part[at, own, :]

    def settle(k):
        with jax.named_scope("w_swap%d" % k):
            swaps[k].wait_recv()
        for side in range(2):
            @pl.when(x == side)
            def _():
                lo = (1 - side) * half + k * part_cols
                out_ref[:, lo:lo + part_cols] = swap_in[k].astype(F32)

    gain_zs = [
        copy(gain_sum, gain_z.at[step], g_send.at[2 + step], g_recv.at[2 + step], z_peers[step])
        for step in range(planes - 1)
    ]
    reach = {}

    def begin(i, k):
        products(i, k)
        reach[i, k] = 1
        stage(0, i, k)

    def advance(i, k):
        if reach[i, k] <= planes - 2 - i:
            stage(reach[i, k], i, k)
            reach[i, k] += 1

    begin(0, 0)

    @pl.when(sec == last)
    def _():
        for b in order[2:]:
            forward_a(b)

    for k in range(2, CHUNKS):
        ux[k].start()
        uy[k].start()
    advance(0, 0)
    begin(0, 1)
    advance(0, 0)
    for i in range(1, pairs):
        begin(i, 0)
        begin(i, 1)
    advance(0, 1)
    for k in range(2, CHUNKS):
        forward_u(k)
    arrive("gain_x", gain_x)
    gain_mid[...] = gain_own[...] + gain_in[0]
    gain_y.start()
    for i in range(1, pairs):
        advance(i, 0)
    advance(0, 1)
    for i in range(1, pairs):
        advance(i, 1)
    for k in range(2, CHUNKS, 2):
        begin(0, k)
        begin(0, k + 1)
        advance(0, k)
        for i in range(1, pairs):
            begin(i, k)
        advance(0, k + 1)
        for i in range(1, pairs):
            begin(i, k + 1)
        if k == 2:
            arrive("gain_y", gain_y)
            gain_sum[...] = gain_mid[...] + gain_in[1]
            for tiny in gain_zs:
                tiny.start()
    finish(0)
    done = 1
    while any(reach[i, k] <= planes - 2 - i for i, k in reach):
        for i, k in block_order(planes, CHUNKS):
            advance(i, k)
        if done < CHUNKS - 2:
            finish(done)
            settle(done - 1)
            done += 1
    for k in range(done, CHUNKS):
        finish(k)
        if k < CHUNKS - 1:
            settle(k - 1)
    for sent in [gain_x, gain_y] + ux + uy + ud + ax + ay + ad + gain_zs:
        sent.wait_send()
    for k in range(CHUNKS):
        for d in range(planes):
            @pl.when(d > z)
            def _():
                right(k * planes + d).wait_send()

            @pl.when(d < z)
            def _():
                left(k * planes + d).wait_send()

    settle(CHUNKS - 2)
    with jax.named_scope("w_gain"):
        for tiny in gain_zs:
            tiny.wait_recv()
    total_gain = gain_sum[...]
    for step in range(planes - 1):
        total_gain = total_gain + gain_z[step]
    gain_z[0] = total_gain
    for r in range(total):
        @pl.when(me == r)
        def _():
            gain_out[...] = gain_z[0, :, r * (channels // total):(r + 1) * (channels // total)]
    settle(CHUNKS - 1)

    for sent in swaps:
        sent.wait_send()

    @pl.when(sec > 0)
    def _():
        for mb in range(micro):
            relay(mb).wait_send()


def store_kernel(*refs):
    count = (len(refs) - 1) // 2
    sems = refs[-1]
    copies = [
        pltpu.make_async_copy(refs[n], refs[count + n], sems.at[n]) for n in range(count)
    ]
    for one in copies:
        one.start()
    for one in copies:
        one.wait()


def body(section_inputs, mix_weight, norm_gain, out_cotangent, positions):
    sections = lax.axis_size("section")
    micro, tok_mb, channels = section_inputs.shape[1:]
    tokens = micro * tok_mb
    count = lax.axis_size("dp")
    planes = count // 4
    share = channels // count
    half = channels // 2
    rows = half // planes
    vmem = pl.BlockSpec(memory_space=pltpu.VMEM)
    hbm = pl.BlockSpec(memory_space=pltpu.HBM)
    part_cols = half // CHUNKS
    hops = CHUNKS * planes
    block = (hops, rows, part_cols)
    line = (1, channels)
    sems = pltpu.SemaphoreType.DMA
    results = pl.pallas_call(
        functools.partial(back_kernel, planes, sections),
        out_shape=(
            jax.ShapeDtypeStruct((share, channels), F32),
            jax.ShapeDtypeStruct((1, share), F32),
            jax.ShapeDtypeStruct((tokens, channels), BF16),
        ),
        in_specs=[hbm] * 5,
        out_specs=(vmem, vmem, vmem),
        scratch_shapes=[
            pltpu.VMEM((tokens, channels), BF16),
            pltpu.VMEM((channels, channels), BF16),
            pltpu.VMEM((tokens, channels), BF16),
            pltpu.VMEM(line, F32),
            pltpu.VMEM((micro, tok_mb), jnp.int32),
            pltpu.VMEM((tokens, channels), F32),
            pltpu.VMEM((2, tokens, rows), BF16),
            pltpu.VMEM((rows, rows), BF16),
            pltpu.VMEM((2, half, tokens), BF16),
            pltpu.VMEM((2 * CHUNKS, tokens, part_cols), BF16),
            pltpu.VMEM((tokens, 128), F32),
            pltpu.VMEM((tokens, 128), F32),
            pltpu.VMEM((tokens, 128), F32),
            pltpu.VMEM((3, half, tokens), BF16),
            pltpu.VMEM((3 * CHUNKS, tokens, part_cols), BF16),
            pltpu.VMEM(block, F32),
            pltpu.VMEM(block, BF16),
            pltpu.VMEM(block, BF16),
            pltpu.VMEM(block, BF16),
            pltpu.VMEM(block, BF16),
            pltpu.VMEM((CHUNKS, share, part_cols), BF16),
            pltpu.VMEM((CHUNKS, share, part_cols), BF16),
            pltpu.VMEM(line, F32),
            pltpu.VMEM((2,) + line, F32),
            pltpu.VMEM(line, F32),
            pltpu.VMEM(line, F32),
            pltpu.VMEM((planes - 1,) + line, F32),
            sems((5,)), sems((micro,)), sems((micro,)),
            sems((3 * CHUNKS,)), sems((3 * CHUNKS,)), sems((3 * planes,)), sems((3 * planes,)),
            sems((CHUNKS,)), sems((CHUNKS,)), sems((hops,)), sems((hops,)),
            sems((hops,)), sems((hops,)), sems((planes + 1,)), sems((planes + 1,)),
        ],
        compiler_params=pltpu.CompilerParams(
            collective_id=0, has_side_effects=True, vmem_limit_bytes=GRANT << 10
        ),
    )(
        section_inputs.reshape(tokens, channels),
        mix_weight[0],
        out_cotangent.reshape(tokens, channels),
        norm_gain,
        positions,
    )
    weight_grad, gain_share, grads = pl.pallas_call(
        store_kernel,
        out_shape=tuple(jax.ShapeDtypeStruct(r.shape, r.dtype) for r in results),
        in_specs=[vmem] * 3,
        out_specs=(hbm,) * 3,
        scratch_shapes=[sems((3,))],
        compiler_params=pltpu.CompilerParams(vmem_limit_bytes=4 << 20),
    )(*results)
    return (grads.reshape(1, micro, tok_mb, channels), weight_grad[None], gain_share)


def solution(mesh):
    return jax.shard_map(
        body,
        mesh=mesh,
        in_specs=(
            P("section", None, "dp", None),
            P("section", None, None),
            P("section", None),
            P(None, "dp", None),
            P(None, "dp"),
        ),
        out_specs=(P("section", None, "dp", None), P("section", "dp", None), P("section", "dp")),
        check_vma=False,
    )
```
